512 devices in a mesh: var: 64 (over x, y_hi, z), samp: 8 (over y_lo, core).
Axes of the slice: x: 4, y: 8 (y_hi: 2, y_lo: 4; y = y_hi * 4 + y_lo), z: 8, core: 2. Of those that a mesh axis runs over, the one named last changes fastest.
Arguments:
- data: float32 [2048, 32768], P('samp', 'var'), may hold values from -6 to 6
- tiles: float32 [64, 3, 512, 512], P('var'), as said below
- offsets: int32 [64, 3], P('var'), may hold values from 0 to 5, as said below
- step: float32 [1], replicated, may hold values from 0.3 to 0.7
Outputs:
- new_tiles: float32 [64, 3, 512, 512], P('var', None, 'samp')
The draws below stay inside these ranges and needn't reach their ends.
Inputs may be any that keep to these rules, and one draw needn't show every extreme that they name: Slot 0 of every block row has offset 0. Every other slot holds 0 (empty) or an offset of 1 to 5; live slots come first in a row and their offsets differ. Some block row has all 3 slots live, one of them at offset 5. `tiles`: tiles of empty slots are zero. Slot 0 is symmetric with its diagonal between 1 and 2.
All inputs are finite; a program needn't handle non-finite values.
Results may differ from the reference program's by a relative error of at most 0.0003.
Values sent between devices are 32-bit elements; how exact they have to be, the bound alone decides.
A program may use at most 64 MiB of HBM per device.

```python
import jax
import jax.numpy as jnp
from jax import lax

BLOCK = 512
MOST = 3
BAND = 6
VARS = 32768
SAMPLES = 2048
N_VAR = 64


def offsets_table(key):
    base = jax.random.fold_in(key, 101)
    first_key, second_key, perm_key, full_key, short_key = jax.random.split(base, 5)
    extra_tiles = jnp.minimum(jax.random.randint(first_key, (N_VAR,), 0, MOST), jax.random.randint(second_key, (N_VAR,), 0, MOST))
    full_row = jax.random.randint(full_key, (), 0, N_VAR)
    row_ids = jnp.arange(N_VAR)
    extra_tiles = jnp.where(row_ids == full_row, MOST - 1, extra_tiles)
    shuffled = jax.vmap(lambda subkey: jax.random.permutation(subkey, BAND - 1))(jax.random.split(perm_key, N_VAR)) + 1
    picked = shuffled[:, :MOST - 1]
    shorter = jax.random.permutation(short_key, BAND - 2) + 1
    full_pick = jnp.concatenate([shorter[:MOST - 2], jnp.full((1,), BAND - 1, jnp.int32)]).astype(jnp.int32)
    picked = jnp.where((row_ids == full_row)[:, None], full_pick[None, :], picked)
    slot_ids = jnp.arange(1, MOST)
    live_slots = slot_ids[None, :] <= extra_tiles[:, None]
    rest = jnp.where(live_slots, picked, 0)
    return jnp.concatenate([jnp.zeros((N_VAR, 1), jnp.int32), rest.astype(jnp.int32)], axis=1).astype(jnp.int32)


def draw_offsets(key, part):
    return offsets_table(key)


def draw_tiles(key, part):
    offset_table = offsets_table(key)
    base = jax.random.fold_in(key, 202)
    entry_key, diag_key = jax.random.split(base, 2)
    shape_full = (N_VAR, MOST, BLOCK, BLOCK)
    entries = 0.04 * jax.random.normal(entry_key, shape_full, jnp.float32)
    diag_values = jax.random.uniform(diag_key, (N_VAR, BLOCK), jnp.float32, 1.0, 2.0)
    first_slot = 0.5 * (entries[:, 0] + jnp.transpose(entries[:, 0], (0, 2, 1)))
    diag_mask = jnp.eye(BLOCK, dtype=bool)
    first_slot = jnp.where(diag_mask[None], diag_values[:, None, :], first_slot)
    others = entries[:, 1:] * (offset_table[:, 1:] > 0).astype(jnp.float32)[:, :, None, None]
    return jnp.concatenate([first_slot[:, None], others], axis=1)


def level_of(rng, dims, cuts, low, largest):
    level = 1.0
    for position, blocks in cuts:
        draws = jax.random.uniform(jax.random.fold_in(jax.random.fold_in(rng, 6), position), (blocks,), jnp.float32, low / len(cuts), largest / len(cuts))
        level = level * jnp.repeat(jnp.exp(draws), dims[position] // blocks).reshape((-1,) + (1,) * (len(dims) - 1 - position))
    return level


def noise(stream_key, extent, width, reach, cuts=(), kind=jnp.bfloat16):
    drawn = jax.random.normal(stream_key, extent, jnp.float32) * width
    if len(cuts) > 0:
        drawn = level_of(stream_key, extent, cuts, -0.22, 0.18) * drawn
    return jnp.clip(drawn, min=-reach, max=reach).astype(kind)


def setup_inputs(seed: int = 0) -> dict:
    splits = jax.random.split(jax.random.key(seed), 5)
    return {
        "data": noise(splits[0], (SAMPLES, VARS), 1.0, 6.0, ((0, 8), (1, 64)), jnp.float32),
        "tiles": draw_tiles(jax.random.fold_in(splits[4], 71), 0),
        "offsets": draw_offsets(jax.random.fold_in(splits[4], 71), 0),
        "step": jnp.clip(jax.random.uniform(splits[3], (1,), jnp.float32, 0.3, 0.7), 0.3, 0.7),
    }


highest = lax.Precision.HIGHEST
penalty_weight = 0.05


def matmul(left_op, right_op):
    return jnp.dot(left_op, right_op, precision=highest, preferred_element_type=jnp.float32)


def columns(array, block_index):
    return lax.dynamic_slice_in_dim(array, (block_index * BLOCK).astype(jnp.int32), BLOCK, 1)


def reference(data, tiles, offsets, step):
    samples = data.shape[0]
    step_size = step[0]

    def add_row(image_acc, block_row):
        for slot_index in range(MOST):
            shift_by = offsets[block_row, slot_index]
            partner = ((block_row + shift_by) % N_VAR).astype(jnp.int32)
            tile_now = tiles[block_row, slot_index]
            live_flag = jnp.where((slot_index == 0) | (shift_by > 0), 1.0, 0.0).astype(jnp.float32)
            mirror = jnp.where(shift_by > 0, 1.0, 0.0).astype(jnp.float32)
            own_block = columns(data, block_row)
            far_block = columns(data, partner)
            forward = matmul(own_block, tile_now) * live_flag
            image_acc = lax.dynamic_update_slice_in_dim(image_acc, columns(image_acc, partner) + forward, (partner * BLOCK).astype(jnp.int32), 1)
            backward = matmul(far_block, tile_now.T) * mirror
            image_acc = lax.dynamic_update_slice_in_dim(image_acc, columns(image_acc, block_row) + backward, (block_row * BLOCK).astype(jnp.int32), 1)
        return image_acc, None

    row_list = jnp.arange(N_VAR, dtype=jnp.int32)
    image_acc, _ = lax.scan(add_row, jnp.zeros(data.shape, jnp.float32), row_list)
    diag_mask = jnp.eye(BLOCK, dtype=bool)

    def new_row(block_row):
        pieces = []
        for slot_index in range(MOST):
            shift_by = offsets[block_row, slot_index]
            partner = ((block_row + shift_by) % N_VAR).astype(jnp.int32)
            tile_now = tiles[block_row, slot_index]
            live_flag = jnp.where((slot_index == 0) | (shift_by > 0), 1.0, 0.0).astype(jnp.float32)
            own_block = columns(data, block_row)
            far_block = columns(data, partner)
            left_term = matmul(own_block.T, columns(image_acc, partner))
            right_term = matmul(columns(image_acc, block_row).T, far_block)
            gradient = (left_term + right_term) / (2.0 * samples)
            if slot_index == 0:
                gradient = gradient - jnp.where(diag_mask, (1.0 / jnp.diagonal(tile_now))[None, :], 0.0)
            stepped = tile_now - step_size * gradient
            shrunk = jnp.sign(stepped) * jnp.maximum(jnp.abs(stepped) - step_size * penalty_weight, 0.0)
            if slot_index == 0:
                shrunk = jnp.where(diag_mask, stepped, shrunk)
            pieces.append(shrunk * live_flag)
        return jnp.stack(pieces)

    return lax.map(new_row, row_list)
```

```python
import functools
import jax
import jax.numpy as jnp
from jax import lax
from jax.experimental import pallas as pl
from jax.experimental.pallas import tpu as pltpu
from jax.sharding import PartitionSpec as P

BAND = 6
MESH = pl.DeviceIdType.MESH
RING = 8
WRAP = 2
CHUNKS = 4


def var_device(index):
    return {"var": index}


def band_kernel(wrap, chunks, reduce_too, *refs):
    if reduce_too:
        (data_ref, first_ref, second_ref, mask_ref, ahead_ref, carried_ref,
         sent_ref, near_ref, far_ref, cross_ref,
         d_send, d_recv, d_direct, d_back,
         c_send, c_near, c_far, c_cross) = refs
    else:
        data_ref, ahead_ref, d_send, d_recv, d_direct, d_back = refs
    count = lax.axis_size("var")
    me = lax.axis_index("var")
    z = lax.rem(me, RING)
    before, after = lax.rem(me + count - 1, count), lax.rem(me + 1, count)
    left5, right5 = lax.rem(me + count - 5, count), lax.rem(me + 5, count)
    rows = data_ref.shape[0] // chunks
    edge = 7 + wrap

    barrier = pltpu.get_barrier_semaphore()
    for other in (before, after, left5, right5):
        pl.semaphore_signal(barrier, inc=1, device_id=var_device(other), device_id_type=MESH)
    pl.semaphore_wait(barrier, 4)

    def part(k):
        return pl.ds(pl.multiple_of(k * rows, rows), rows)

    def natural(t, k):
        source = data_ref.at[part(k)] if t == 0 else ahead_ref.at[t - 1, part(k)]
        return pltpu.make_async_remote_copy(
            src_ref=source, dst_ref=ahead_ref.at[t, part(k)],
            send_sem=d_send.at[t, k], recv_sem=d_recv.at[t, k],
            device_id=var_device(before), device_id_type=MESH)

    def direct(k):
        return pltpu.make_async_remote_copy(
            src_ref=data_ref.at[part(k)], dst_ref=ahead_ref.at[4, part(k)],
            send_sem=d_direct.at[k], recv_sem=d_recv.at[4, k],
            device_id=var_device(left5), device_id_type=MESH)

    def back(t, k):
        return pltpu.make_async_remote_copy(
            src_ref=ahead_ref.at[t - 1, part(k)], dst_ref=ahead_ref.at[t - 2, part(k)],
            send_sem=d_back.at[t - 2, k], recv_sem=d_recv.at[t - 2, k],
            device_id=var_device(after), device_id_type=MESH)

    def goes_on(t):
        return ((z >= 1) & (z + t <= edge)) | ((z == 0) & (t + 1 <= wrap))

    sends_direct = (z >= wrap) & (z <= 4)

    def arrived(t, k):
        natural(t - 1, k).wait_recv()

    def own(o, k):
        return mask_ref[2 * o : 2 * o + 1] * first_ref[part(k)] + mask_ref[2 * o + 1 : 2 * o + 2] * second_ref[part(k)]

    def pass_on(o, k):
        return pltpu.make_async_remote_copy(
            src_ref=sent_ref.at[o - 1, part(k)], dst_ref=near_ref.at[o - 1, part(k)],
            send_sem=c_send.at[o - 1, k], recv_sem=c_near.at[o - 1, k],
            device_id=var_device(after), device_id_type=MESH)

    def pass_back(o, k):
        return pltpu.make_async_remote_copy(
            src_ref=sent_ref.at[o - 1, part(k)], dst_ref=far_ref.at[o, part(k)],
            send_sem=c_send.at[o - 1, k], recv_sem=c_far.at[o, k],
            device_id=var_device(before), device_id_type=MESH)

    def pass_cross(k):
        return pltpu.make_async_remote_copy(
            src_ref=sent_ref.at[4, part(k)], dst_ref=cross_ref.at[part(k)],
            send_sem=c_send.at[4, k], recv_sem=c_cross.at[k],
            device_id=var_device(right5), device_id_type=MESH)

    def passes(o):
        return ((z <= 6) & (z + o <= edge)) | ((z == 7) & (o <= wrap))

    def has_near(o):
        return (o < 5) & (((z >= 1) & (z + o <= edge)) | ((z == 0) & (o + 1 <= wrap)))

    def loop(body):
        def step(k, carry):
            body(k)
            return carry
        lax.fori_loop(0, chunks, step, 0)

    def first(k):
        natural(0, k).start()

        @pl.when(sends_direct)
        def _():
            direct(k).start()

        if reduce_too:
            sent_ref[4, part(k)] = own(5, k)

            @pl.when(passes(5))
            def _():
                pass_on(5, k).start()

            @pl.when(z == 7)
            def _():
                for o in range(wrap + 1, 5):
                    sent_ref[o - 1, part(k)] = own(o, k)
                    pass_back(o, k).start()
                if wrap < 5:
                    pass_cross(k).start()

    loop(first)

    for tau in range(1, 6):
        cross_t = 7 - tau

        def step(k, tau=tau, cross_t=cross_t):
            @pl.when(z + tau <= edge)
            def _():
                arrived(tau, k)

            if tau <= 4:
                @pl.when(goes_on(tau))
                def _():
                    natural(tau, k).start()

            if reduce_too and tau <= 4:
                o = 5 - tau

                @pl.when(passes(o))
                def _():
                    @pl.when(has_near(o))
                    def _():
                        pass_on(o + 1, k).wait_recv()
                        sent_ref[o - 1, part(k)] = near_ref[o, part(k)] + own(o, k)

                    @pl.when(jnp.logical_not(has_near(o)))
                    def _():
                        sent_ref[o - 1, part(k)] = own(o, k)

                    pass_on(o, k).start()

            if reduce_too and tau <= 4:
                place = 7 - tau
                for o in range(wrap + 1 + tau, 6):
                    @pl.when(z == place)
                    def _(o=o):
                        pass_back(o - 1, k).wait_recv()
                        sent_ref[o - 1, part(k)] = far_ref[o - 1, part(k)] + own(o, k)
                        if o < 5:
                            pass_back(o, k).start()
                        else:
                            pass_cross(k).start()

            if 2 <= tau and cross_t > wrap:
                @pl.when(z + cross_t > edge)
                def _():
                    arrived(cross_t, k)
                    if cross_t >= 2:
                        @pl.when(z <= 6)
                        def _():
                            back(cross_t, k).start()

        loop(step)

    if reduce_too:
        def final(k):
            pass_on(1, k).wait_recv()
            carried_ref[part(k)] = near_ref[0, part(k)]

            @pl.when(sends_direct)
            def _():
                pass_cross(k).wait_recv()
                carried_ref[part(k)] += cross_ref[part(k)]

        loop(final)

    def drain(k):
        natural(0, k).wait_send()

        @pl.when(sends_direct)
        def _():
            direct(k).wait_send()

        for t in range(1, 5):
            @pl.when(goes_on(t))
            def _(t=t):
                natural(t, k).wait_send()

        for t in range(wrap + 1, 6):
            if t >= 2:
                @pl.when((z + t > edge) & (z <= 6))
                def _(t=t):
                    back(t, k).wait_send()

        if reduce_too:
            for o in range(1, 6):
                @pl.when(passes(o) | (z + o > edge))
                def _(o=o):
                    pass_on(o, k).wait_send()

    loop(drain)


def band_call(data, sums, masks, wrap, chunks, reduce_too, collective_id):
    rows, size = data.shape
    dtype = data.dtype
    sem = pltpu.SemaphoreType.DMA
    block = jax.ShapeDtypeStruct((rows, size), dtype)
    ahead = jax.ShapeDtypeStruct((5, rows, size), dtype)
    vm = pl.BlockSpec(memory_space=pltpu.VMEM)
    base = [sem((5, chunks)), sem((5, chunks)), sem((chunks,)), sem((4, chunks))]
    if reduce_too:
        scratch = [pltpu.VMEM((5, rows, size), dtype)] * 3 + [pltpu.VMEM((rows, size), dtype)] + base + [
            sem((5, chunks)), sem((5, chunks)), sem((5, chunks)), sem((chunks,))]
        args, outs, specs = (data, *sums, masks), (ahead, block), (vm, vm)
    else:
        scratch, args, outs, specs = base, (data,), ahead, vm
    return pl.pallas_call(
        functools.partial(band_kernel, wrap, chunks, reduce_too),
        out_shape=outs, in_specs=[vm] * len(args), out_specs=specs, scratch_shapes=scratch,
        compiler_params=pltpu.CompilerParams(collective_id=collective_id, has_side_effects=True),
    )(*args)


def sum_kernel(grad_ref, out_ref, pair_ref, sent_ref, up_ref, down_ref,
               p_send, p_recv, u_send, u_recv, d_send, d_recv):
    me = lax.axis_index("samp")
    core = lax.rem(me, 2)
    y = me // 2
    places = lax.axis_size("samp") // 2
    rows = out_ref.shape[1]
    twin = me + 1 - 2 * core

    barrier = pltpu.get_barrier_semaphore()

    def greet(other):
        pl.semaphore_signal(barrier, inc=1, device_id={"samp": other}, device_id_type=MESH)

    greet(twin)

    @pl.when(y < places - 1)
    def _():
        greet(me + 2)

    @pl.when(y > 0)
    def _():
        greet(me - 2)

    peers = 1 + lax.min(y, 1) + lax.min(places - 1 - y, 1)
    pl.semaphore_wait(barrier, peers)

    def band(place, which):
        return pl.ds(pl.multiple_of((2 * place + which) * rows, rows), rows)

    def to_twin(place):
        return pltpu.make_async_remote_copy(
            src_ref=grad_ref.at[:, band(place, 1 - core)], dst_ref=pair_ref.at[place],
            send_sem=p_send.at[place], recv_sem=p_recv.at[place],
            device_id={"samp": twin}, device_id_type=MESH)

    def up(place):
        return pltpu.make_async_remote_copy(
            src_ref=sent_ref.at[place], dst_ref=up_ref.at[place],
            send_sem=u_send.at[place], recv_sem=u_recv.at[place],
            device_id={"samp": me + 2}, device_id_type=MESH)

    def down(place):
        return pltpu.make_async_remote_copy(
            src_ref=sent_ref.at[place], dst_ref=down_ref.at[place],
            send_sem=d_send.at[place], recv_sem=d_recv.at[place],
            device_id={"samp": me - 2}, device_id_type=MESH)

    order = []
    for j in range(places - 1):
        order += [places - 1 - j, j]
    starts = list(dict.fromkeys(order))
    for place in starts:
        to_twin(place).start()

    for j in range(places - 1):
        for rising in (True, False):
            place = places - 1 - j if rising else j

            @pl.when(y < place if rising else y > place)
            def _(place=place, rising=rising):
                to_twin(place).wait_recv()
                sent_ref[place] = grad_ref[:, band(place, core)] + pair_ref[place]

                @pl.when(y > 0 if rising else y < places - 1)
                def _():
                    if rising:
                        up(place).wait_recv()
                        sent_ref[place] += up_ref[place]
                    else:
                        down(place).wait_recv()
                        sent_ref[place] += down_ref[place]

                (up if rising else down)(place).start()

    for place in range(places):
        @pl.when(y == place)
        def _(place=place):
            to_twin(place).wait_recv()
            out_ref[...] = grad_ref[:, band(place, core)] + pair_ref[place]
            if place > 0:
                up(place).wait_recv()
                out_ref[...] += up_ref[place]
            if place < places - 1:
                down(place).wait_recv()
                out_ref[...] += down_ref[place]

    for place in range(places):
        to_twin(place).wait_send()

        @pl.when(y < place)
        def _(place=place):
            up(place).wait_send()

        @pl.when(y > place)
        def _(place=place):
            down(place).wait_send()


def sum_call(grad, collective_id):
    slots, size, width = grad.shape
    count = lax.axis_size("samp")
    rows = size // count
    sem = pltpu.SemaphoreType.DMA
    vm = pl.BlockSpec(memory_space=pltpu.VMEM)
    places = count // 2
    buffer = pltpu.VMEM((places, slots, rows, width), grad.dtype)
    return pl.pallas_call(
        sum_kernel,
        out_shape=jax.ShapeDtypeStruct((slots, rows, width), grad.dtype),
        in_specs=[vm], out_specs=vm,
        scratch_shapes=[buffer] * 4 + [sem((places,))] * 6,
        compiler_params=pltpu.CompilerParams(collective_id=collective_id, has_side_effects=True),
    )(grad)


high = lax.Precision.HIGH
penalty_weight = 0.05


def product(left, right, left_dim, right_dim):
    return lax.dot_general(left, right, (((left_dim,), (right_dim,)), ((), ())),
                           precision=high, preferred_element_type=jnp.float32)


def picked(offset, own, ahead):
    block = own
    for o in range(1, BAND):
        block = jnp.where(offset == o, ahead[o - 1], block)
    return block


def shards(data, tiles, offsets, step):
    tiles = tiles[0]
    offset = offsets[0]
    slots, size = tiles.shape[0], tiles.shape[1]
    samp_count = lax.axis_size("samp")
    samples = data.shape[0] * samp_count
    step_size = step[0]
    forward = [product(data, tiles[j], 1, 0) for j in range(slots)]
    places = jnp.arange(16) // 2
    slot_of_row = 1 + jnp.arange(16) % 2
    live = ((offset[slot_of_row] == places) & (places > 0)).astype(jnp.float32)
    masks = jnp.broadcast_to(live[:, None], (16, size))
    ahead, carried = band_call(data, forward[1:], masks, WRAP, CHUNKS, True, 1)
    partners = [data] + [picked(offset[j], data, ahead) for j in range(1, slots)]
    image = forward[0] + carried
    for j in range(1, slots):
        image = image + product(partners[j], tiles[j], 1, 1)
    image_ahead = band_call(image, None, None, WRAP, CHUNKS, False, 2)
    image_partners = [image] + [picked(offset[j], image, image_ahead) for j in range(1, slots)]
    grad = jnp.stack([product(data, image_partners[j], 0, 0) + product(image, partners[j], 0, 0) for j in range(slots)])
    summed = sum_call(grad, 3)
    rows = size // samp_count
    row_start = lax.axis_index("samp") * rows
    old = lax.dynamic_slice_in_dim(tiles, row_start, rows, 1)
    slot_ids = jnp.arange(slots)
    on_diag = (row_start + jnp.arange(rows))[:, None] == jnp.arange(size)[None, :]
    diag = on_diag[None] & (slot_ids == 0)[:, None, None]
    gradient = summed / (2.0 * samples) - jnp.where(diag, 1.0 / jnp.where(diag, old, 1.0), 0.0)
    stepped = old - step_size * gradient
    shrunk = jnp.sign(stepped) * jnp.maximum(jnp.abs(stepped) - step_size * penalty_weight, 0.0)
    active = (slot_ids == 0) | (offset > 0)
    return jnp.where(active[:, None, None], jnp.where(diag, stepped, shrunk), 0.0)[None]


def solution(mesh):
    return jax.shard_map(
        shards,
        mesh=mesh,
        in_specs=(P("samp", "var"), P("var", None, None, None), P("var", None), P()),
        out_specs=P("var", None, "samp", None),
        check_vma=False,
    )
```

```python
import functools
import jax
import jax.numpy as jnp
from jax import lax
from jax.experimental import pallas as pl
from jax.experimental.pallas import tpu as pltpu
from jax.sharding import PartitionSpec as P

BAND = 6
MESH = pl.DeviceIdType.MESH
RING = 8
WRAP = 2
CHUNKS = 4
PENALTY = 0.05


def halves(x):
    top = x.astype(jnp.bfloat16)
    return top, (x - top.astype(jnp.float32)).astype(jnp.bfloat16)


def product(left, right, left_dim, right_dim):
    def dot(a, b):
        return lax.dot_general(a, b, (((left_dim,), (right_dim,)), ((), ())), preferred_element_type=jnp.float32)

    return dot(left[0], right[0]) + dot(left[0], right[1]) + dot(left[1], right[0])


def var_device(index):
    return {"var": index}


def band_kernel(wrap, chunks, reduce_too, *refs):
    if reduce_too:
        (offset_ref, data_ref, tiles_ref, image_ref, picked_ref,
         ahead_ref, first_ref, second_ref, top_ref, rest_ref, sent_ref, near_ref, far_ref, cross_ref,
         d_send, d_recv, d_direct, d_back,
         c_send, c_near, c_far, c_cross) = refs
    else:
        offset_ref, data_ref, picked_ref, ahead_ref, d_send, d_recv, d_direct, d_back = refs
    count = lax.axis_size("var")
    me = lax.axis_index("var")
    z = lax.rem(me, RING)
    before, after = lax.rem(me + count - 1, count), lax.rem(me + 1, count)
    left5, right5 = lax.rem(me + count - 5, count), lax.rem(me + 5, count)
    rows = data_ref.shape[0] // chunks
    edge = 7 + wrap

    barrier = pltpu.get_barrier_semaphore()
    for other in (before, after, left5, right5):
        pl.semaphore_signal(barrier, inc=1, device_id=var_device(other), device_id_type=MESH)
    pl.semaphore_wait(barrier, 4)

    def part(k):
        return pl.ds(pl.multiple_of(k * rows, rows), rows)

    def natural(t, k):
        source = data_ref.at[part(k)] if t == 0 else ahead_ref.at[t - 1, part(k)]
        return pltpu.make_async_remote_copy(
            src_ref=source, dst_ref=ahead_ref.at[t, part(k)],
            send_sem=d_send.at[t, k], recv_sem=d_recv.at[t, k],
            device_id=var_device(before), device_id_type=MESH)

    def direct(k):
        return pltpu.make_async_remote_copy(
            src_ref=data_ref.at[part(k)], dst_ref=ahead_ref.at[4, part(k)],
            send_sem=d_direct.at[k], recv_sem=d_recv.at[4, k],
            device_id=var_device(left5), device_id_type=MESH)

    def back(t, k):
        return pltpu.make_async_remote_copy(
            src_ref=ahead_ref.at[t - 1, part(k)], dst_ref=ahead_ref.at[t - 2, part(k)],
            send_sem=d_back.at[t - 2, k], recv_sem=d_recv.at[t - 2, k],
            device_id=var_device(after), device_id_type=MESH)

    def goes_on(t):
        return ((z >= 1) & (z + t <= edge)) | ((z == 0) & (t + 1 <= wrap))

    sends_direct = (z >= wrap) & (z <= 4)

    def arrived(t, k):
        natural(t - 1, k).wait_recv()

    def chosen(slot, o):
        return jnp.where(offset_ref[0, slot] == o, 1.0, 0.0)

    def own(o, k):
        return chosen(1, o) * first_ref[part(k)] + chosen(2, o) * second_ref[part(k)]

    def pick(k):
        for slot in (1, 2):
            block = chosen(slot, 1) * ahead_ref[0, part(k)]
            for o in range(2, BAND):
                block += chosen(slot, o) * ahead_ref[o - 1, part(k)]
            picked_ref[slot - 1, part(k)] = block

    def pass_on(o, k):
        return pltpu.make_async_remote_copy(
            src_ref=sent_ref.at[o - 1, part(k)], dst_ref=near_ref.at[o - 1, part(k)],
            send_sem=c_send.at[o - 1, k], recv_sem=c_near.at[o - 1, k],
            device_id=var_device(after), device_id_type=MESH)

    def pass_back(o, k):
        return pltpu.make_async_remote_copy(
            src_ref=sent_ref.at[o - 1, part(k)], dst_ref=far_ref.at[o, part(k)],
            send_sem=c_send.at[o - 1, k], recv_sem=c_far.at[o, k],
            device_id=var_device(before), device_id_type=MESH)

    def pass_cross(k):
        return pltpu.make_async_remote_copy(
            src_ref=sent_ref.at[4, part(k)], dst_ref=cross_ref.at[part(k)],
            send_sem=c_send.at[4, k], recv_sem=c_cross.at[k],
            device_id=var_device(right5), device_id_type=MESH)

    def passes(o):
        return ((z <= 6) & (z + o <= edge)) | ((z == 7) & (o <= wrap))

    def loop(body):
        def step(k, carry):
            body(k)
            return carry
        lax.fori_loop(0, chunks, step, 0)

    def first(k):
        natural(0, k).start()

        @pl.when(sends_direct)
        def _():
            direct(k).start()

    loop(first)

    if reduce_too:
        for slot in range(3):
            top, rest = halves(tiles_ref[slot])
            top_ref[slot] = top
            rest_ref[slot] = rest

        def forward(k):
            mine = halves(data_ref[part(k)])
            first_ref[part(k)] = product(mine, (top_ref[1], rest_ref[1]), 1, 0)
            second_ref[part(k)] = product(mine, (top_ref[2], rest_ref[2]), 1, 0)
            sent_ref[4, part(k)] = own(5, k)

            @pl.when(passes(5))
            def _():
                pass_on(5, k).start()

            @pl.when(z == 7)
            def _():
                for o in range(wrap + 1, 5):
                    sent_ref[o - 1, part(k)] = own(o, k)
                    pass_back(o, k).start()
                pass_cross(k).start()

        loop(forward)

        def diagonal(k):
            image_ref[part(k)] = product(halves(data_ref[part(k)]), (top_ref[0], rest_ref[0]), 1, 0)

        loop(diagonal)

    for tau in range(1, 6):
        def step(k, tau=tau):
            if reduce_too and tau <= 4:
                o = lax.min(4, edge - z) + 1 - tau

                @pl.when(o >= 1)
                def _():
                    @pl.when((z >= 1) | (o + 1 <= wrap))
                    def _():
                        pass_on(o + 1, k).wait_recv()
                        sent_ref[o - 1, part(k)] = near_ref[o, part(k)] + own(o, k)

                    @pl.when((z == 0) & (o + 1 > wrap))
                    def _():
                        sent_ref[o - 1, part(k)] = own(o, k)

                    pass_on(o, k).start()

            @pl.when(z + tau <= edge)
            def _():
                arrived(tau, k)

            if tau <= 4:
                @pl.when(goes_on(tau))
                def _():
                    natural(tau, k).start()

            if reduce_too and tau <= 4:
                place = 7 - tau
                for o in range(wrap + 1 + tau, 6):
                    @pl.when(z == place)
                    def _(o=o):
                        pass_back(o - 1, k).wait_recv()
                        sent_ref[o - 1, part(k)] = far_ref[o - 1, part(k)] + own(o, k)
                        if o < 5:
                            pass_back(o, k).start()
                        else:
                            pass_cross(k).start()

            for t in {2: (5, 4), 4: (3,), 5: (2,)}.get(tau, ()):
                if t > wrap:
                    @pl.when(z + t > edge)
                    def _(t=t):
                        arrived(t, k)

                        @pl.when(z <= 6)
                        def _():
                            back(t, k).start()

        loop(step)

    if reduce_too:
        def final(k):
            pick(k)
            pass_on(1, k).wait_recv()
            total = image_ref[part(k)] + near_ref[0, part(k)]
            for slot in (1, 2):
                total += product(halves(picked_ref[slot - 1, part(k)]), (top_ref[slot], rest_ref[slot]), 1, 1)
            image_ref[part(k)] = total

            @pl.when(sends_direct)
            def _():
                pass_cross(k).wait_recv()
                image_ref[part(k)] += cross_ref[part(k)]

        loop(final)
    else:
        loop(pick)

    def drain(k):
        natural(0, k).wait_send()

        @pl.when(sends_direct)
        def _():
            direct(k).wait_send()

        for t in range(1, 5):
            @pl.when(goes_on(t))
            def _(t=t):
                natural(t, k).wait_send()

        for t in range(wrap + 1, 6):
            if t >= 2:
                @pl.when((z + t > edge) & (z <= 6))
                def _(t=t):
                    back(t, k).wait_send()

        if reduce_too:
            for o in range(1, 6):
                @pl.when(passes(o) | (z + o > edge))
                def _(o=o):
                    pass_on(o, k).wait_send()

    loop(drain)


def band_call(offsets, data, tiles, wrap, chunks, collective_id):
    reduce_too = tiles is not None
    rows, size = data.shape
    dtype = data.dtype
    sem = pltpu.SemaphoreType.DMA
    vm = pl.BlockSpec(memory_space=pltpu.VMEM)
    sm = pl.BlockSpec(memory_space=pltpu.SMEM)
    block = pltpu.VMEM((rows, size), dtype)
    five = pltpu.VMEM((5, rows, size), dtype)
    picked = jax.ShapeDtypeStruct((2, rows, size), dtype)
    base = [sem((5, chunks)), sem((5, chunks)), sem((chunks,)), sem((4, chunks))]
    if reduce_too:
        halved = pltpu.VMEM(tiles.shape, jnp.bfloat16)
        scratch = [five, block, block, halved, halved, five, five, five, block] + base + [
            sem((5, chunks)), sem((5, chunks)), sem((5, chunks)), sem((chunks,))]
        args, ins = (offsets, data, tiles), [sm, vm, vm]
        outs, specs = (jax.ShapeDtypeStruct((rows, size), dtype), picked), (vm, vm)
    else:
        scratch = [five] + base
        args, ins, outs, specs = (offsets, data), [sm, vm], picked, vm
    return pl.pallas_call(
        functools.partial(band_kernel, wrap, chunks, reduce_too),
        out_shape=outs, in_specs=ins, out_specs=specs, scratch_shapes=scratch,
        compiler_params=pltpu.CompilerParams(collective_id=collective_id, has_side_effects=True),
    )(*args)


def step_kernel(samples, offset_ref, step_ref, data_ref, image_ref, near_ref, later_ref, tiles_ref, out_ref,
               grad_ref, pair_ref, sent_ref, up_ref, down_ref,
               p_send, p_recv, u_send, u_recv, d_send, d_recv):
    me = lax.axis_index("samp")
    core = lax.rem(me, 2)
    y = me // 2
    places = lax.axis_size("samp") // 2
    rows = out_ref.shape[1]
    twin = me + 1 - 2 * core

    barrier = pltpu.get_barrier_semaphore()

    def greet(other):
        pl.semaphore_signal(barrier, inc=1, device_id={"samp": other}, device_id_type=MESH)

    greet(twin)

    @pl.when(y < places - 1)
    def _():
        greet(me + 2)

    @pl.when(y > 0)
    def _():
        greet(me - 2)

    peers = 1 + lax.min(y, 1) + lax.min(places - 1 - y, 1)
    pl.semaphore_wait(barrier, peers)

    def band(place, which):
        return pl.ds(pl.multiple_of((2 * place + which) * rows, rows), rows)

    def to_twin(place):
        return pltpu.make_async_remote_copy(
            src_ref=grad_ref.at[:, band(place, 1 - core)], dst_ref=pair_ref.at[place],
            send_sem=p_send.at[place], recv_sem=p_recv.at[place],
            device_id={"samp": twin}, device_id_type=MESH)

    def up(place):
        return pltpu.make_async_remote_copy(
            src_ref=sent_ref.at[place], dst_ref=up_ref.at[place],
            send_sem=u_send.at[place], recv_sem=u_recv.at[place],
            device_id={"samp": me + 2}, device_id_type=MESH)

    def down(place):
        return pltpu.make_async_remote_copy(
            src_ref=sent_ref.at[place], dst_ref=down_ref.at[place],
            send_sem=d_send.at[place], recv_sem=d_recv.at[place],
            device_id={"samp": me - 2}, device_id_type=MESH)

    order = []
    for j in range(places - 1):
        order += [places - 1 - j, j]
    starts = list(dict.fromkeys(order))
    width = 2 * rows
    data, image = halves(data_ref[...]), halves(image_ref[...])
    rights = [(image, data)] + [(halves(later_ref[j]), halves(near_ref[j])) for j in range(2)]
    for place in starts:
        span = slice(width * place, width * (place + 1))
        for slot, (right_image, right_data) in enumerate(rights):
            grad_ref[slot, span] = (
                product([h[:, span] for h in data], right_image, 0, 0)
                + product([h[:, span] for h in image], right_data, 0, 0))
        to_twin(place).start()

    for j in range(places - 1):
        for rising in (True, False):
            place = places - 1 - j if rising else j

            @pl.when(y < place if rising else y > place)
            def _(place=place, rising=rising):
                to_twin(place).wait_recv()
                sent_ref[place] = grad_ref[:, band(place, core)] + pair_ref[place]

                @pl.when(y > 0 if rising else y < places - 1)
                def _():
                    if rising:
                        up(place).wait_recv()
                        sent_ref[place] += up_ref[place]
                    else:
                        down(place).wait_recv()
                        sent_ref[place] += down_ref[place]

                (up if rising else down)(place).start()

    for place in range(places):
        @pl.when(y == place)
        def _(place=place):
            to_twin(place).wait_recv()
            out_ref[...] = grad_ref[:, band(place, core)] + pair_ref[place]
            if place > 0:
                up(place).wait_recv()
                out_ref[...] += up_ref[place]
            if place < places - 1:
                down(place).wait_recv()
                out_ref[...] += down_ref[place]

    step_size = step_ref[0]
    start = pl.multiple_of(me * rows, rows)
    row_ids = start + lax.broadcasted_iota(jnp.int32, out_ref.shape[1:], 0)
    on_diag = row_ids == lax.broadcasted_iota(jnp.int32, out_ref.shape[1:], 1)
    for slot in range(3):
        old = tiles_ref[slot, pl.ds(start, rows)]
        gradient = out_ref[slot] / (2.0 * samples)
        if slot == 0:
            gradient -= jnp.where(on_diag, 1.0 / jnp.where(on_diag, old, 1.0), 0.0)
        stepped = old - step_size * gradient
        bound = step_size * PENALTY
        shrunk = jnp.where(stepped > bound, stepped - bound, jnp.where(stepped < -bound, stepped + bound, 0.0))
        if slot == 0:
            shrunk = jnp.where(on_diag, stepped, shrunk)
        else:
            shrunk = shrunk * jnp.where(offset_ref[0, slot] > 0, 1.0, 0.0)
        out_ref[slot] = shrunk

    for place in range(places):
        to_twin(place).wait_send()

        @pl.when(y < place)
        def _(place=place):
            up(place).wait_send()

        @pl.when(y > place)
        def _(place=place):
            down(place).wait_send()


def step_call(offsets, step, data, image, near, later, tiles, collective_id):
    slots, size, width = tiles.shape
    count = lax.axis_size("samp")
    rows = size // count
    sem = pltpu.SemaphoreType.DMA
    vm = pl.BlockSpec(memory_space=pltpu.VMEM)
    sm = pl.BlockSpec(memory_space=pltpu.SMEM)
    places = count // 2
    buffer = pltpu.VMEM((places, slots, rows, width), data.dtype)
    return pl.pallas_call(
        functools.partial(step_kernel, data.shape[0] * count),
        out_shape=jax.ShapeDtypeStruct((slots, rows, width), data.dtype),
        in_specs=[sm, sm] + [vm] * 5, out_specs=vm,
        scratch_shapes=[pltpu.VMEM((slots, size, width), data.dtype)] + [buffer] * 4 + [sem((places,))] * 6,
        compiler_params=pltpu.CompilerParams(collective_id=collective_id, has_side_effects=True),
    )(offsets, step, data, image, near, later, tiles)


def shards(data, tiles, offsets, step):
    tiles = tiles[0]
    image, near = band_call(offsets, data, tiles, WRAP, CHUNKS, 1)
    later = band_call(offsets, image, None, WRAP, CHUNKS, 2)
    return step_call(offsets, step, data, image, near, later, tiles, 3)[None]


def solution(mesh):
    return jax.shard_map(
        shards,
        mesh=mesh,
        in_specs=(P("samp", "var"), P("var", None, None, None), P("var", None), P()),
        out_specs=P("var", None, "samp", None),
        check_vma=False,
    )
```

```python
import functools
import jax
import jax.numpy as jnp
from jax import lax
from jax.experimental import pallas as pl
from jax.experimental.pallas import tpu as pltpu
from jax.sharding import PartitionSpec as P

BAND = 6
MESH = pl.DeviceIdType.MESH
RING = 8
WRAP_SUMS = 3
WRAP = 2
CHUNKS = 4
PENALTY = 0.05


def halves(x):
    top = x.astype(jnp.bfloat16)
    return top, (x - top.astype(jnp.float32)).astype(jnp.bfloat16)


def product(left, right, left_dim, right_dim):
    def dot(a, b):
        return lax.dot_general(a, b, (((left_dim,), (right_dim,)), ((), ())), preferred_element_type=jnp.float32)

    return dot(left[0], right[0]) + dot(left[0], right[1]) + dot(left[1], right[0])


def var_device(index):
    return {"var": index}


def band_kernel(wrap, chunks, reduce_too, *refs):
    if reduce_too:
        (offset_ref, data_ref, tiles_ref, image_ref, picked_ref,
         ahead_ref, first_ref, second_ref, top_ref, rest_ref, sent_ref, near_ref, far_ref, cross_ref, relay_ref,
         d_send, d_recv, d_direct, d_back,
         c_send, c_near, c_far, c_cross, d_hold, d_relay) = refs
    else:
        offset_ref, data_ref, picked_ref, ahead_ref, d_send, d_recv, d_direct, d_back = refs
    count = lax.axis_size("var")
    me = lax.axis_index("var")
    z = lax.rem(me, RING)
    before, after = lax.rem(me + count - 1, count), lax.rem(me + 1, count)
    left5, right5 = lax.rem(me + count - 5, count), lax.rem(me + 5, count)
    left6, right6 = lax.rem(me + count - 6, count), lax.rem(me + 6, count)
    rows = data_ref.shape[0] // chunks
    edge = 7 + wrap

    barrier = pltpu.get_barrier_semaphore()
    others = (before, after, left5, right5) + ((left6, right6) if reduce_too else ())
    for other in others:
        pl.semaphore_signal(barrier, inc=1, device_id=var_device(other), device_id_type=MESH)
    pl.semaphore_wait(barrier, len(others))

    def part(k):
        return pl.ds(pl.multiple_of(k * rows, rows), rows)

    def natural(t, k):
        source = data_ref.at[part(k)] if t == 0 else ahead_ref.at[t - 1, part(k)]
        return pltpu.make_async_remote_copy(
            src_ref=source, dst_ref=ahead_ref.at[t, part(k)],
            send_sem=d_send.at[t, k], recv_sem=d_recv.at[t, k],
            device_id=var_device(before), device_id_type=MESH)

    def direct(k):
        return pltpu.make_async_remote_copy(
            src_ref=data_ref.at[part(k)], dst_ref=ahead_ref.at[4, part(k)],
            send_sem=d_direct.at[k], recv_sem=d_recv.at[4, k],
            device_id=var_device(left5), device_id_type=MESH)

    def direct_far(k):
        return pltpu.make_async_remote_copy(
            src_ref=data_ref.at[part(k)], dst_ref=relay_ref.at[part(k)],
            send_sem=d_direct.at[k], recv_sem=d_hold.at[k],
            device_id=var_device(left6), device_id_type=MESH)

    def relay(k):
        return pltpu.make_async_remote_copy(
            src_ref=relay_ref.at[part(k)], dst_ref=ahead_ref.at[4, part(k)],
            send_sem=d_relay.at[k], recv_sem=d_recv.at[4, k],
            device_id=var_device(after), device_id_type=MESH)

    def back(t, k):
        return pltpu.make_async_remote_copy(
            src_ref=ahead_ref.at[t - 1, part(k)], dst_ref=ahead_ref.at[t - 2, part(k)],
            send_sem=d_back.at[t - 2, k], recv_sem=d_recv.at[t - 2, k],
            device_id=var_device(after), device_id_type=MESH)

    def goes_on(t):
        return ((z >= 1) & (z + t <= edge)) | ((z == 0) & (t + 1 <= wrap))

    sends_direct = (z >= wrap) & (z <= 4)

    def arrived(t, k):
        natural(t - 1, k).wait_recv()

    def chosen(slot, o):
        return jnp.where(offset_ref[0, slot] == o, 1.0, 0.0)

    def own(o, k):
        return chosen(1, o) * first_ref[part(k)] + chosen(2, o) * second_ref[part(k)]

    def pick(k):
        for slot in (1, 2):
            block = chosen(slot, 1) * ahead_ref[0, part(k)]
            for o in range(2, BAND):
                block += chosen(slot, o) * ahead_ref[o - 1, part(k)]
            picked_ref[slot - 1, part(k)] = block

    def pass_on(o, k):
        return pltpu.make_async_remote_copy(
            src_ref=sent_ref.at[o - 1, part(k)], dst_ref=near_ref.at[o - 1, part(k)],
            send_sem=c_send.at[o - 1, k], recv_sem=c_near.at[o - 1, k],
            device_id=var_device(after), device_id_type=MESH)

    def pass_back(o, k):
        return pltpu.make_async_remote_copy(
            src_ref=sent_ref.at[o - 1, part(k)], dst_ref=far_ref.at[o, part(k)],
            send_sem=c_send.at[o - 1, k], recv_sem=c_far.at[o, k],
            device_id=var_device(before), device_id_type=MESH)

    def pass_cross(k):
        return pltpu.make_async_remote_copy(
            src_ref=sent_ref.at[4, part(k)], dst_ref=cross_ref.at[part(k)],
            send_sem=c_send.at[4, k], recv_sem=c_cross.at[k],
            device_id=var_device(right5), device_id_type=MESH)

    def passes(o):
        return ((z <= 6) & (z + o <= edge)) | ((z == 7) & (o <= wrap))

    def loop(body):
        def step(k, carry):
            body(k)
            return carry
        lax.fori_loop(0, chunks, step, 0)

    def first(k):
        natural(0, k).start()

        if reduce_too:
            @pl.when((z >= wrap) & (z <= 3))
            def _():
                direct(k).start()

            @pl.when(z == 4)
            def _():
                direct_far(k).start()
        else:
            @pl.when(sends_direct)
            def _():
                direct(k).start()

    loop(first)

    if reduce_too:
        for slot in range(3):
            top, rest = halves(tiles_ref[slot])
            top_ref[slot] = top
            rest_ref[slot] = rest

        mine = halves(data_ref[...])
        first_ref[...] = product(mine, (top_ref[1], rest_ref[1]), 1, 0)
        second_ref[...] = product(mine, (top_ref[2], rest_ref[2]), 1, 0)

        def forward(k):
            sent_ref[4, part(k)] = own(5, k)

            @pl.when(passes(5))
            def _():
                pass_on(5, k).start()

            @pl.when(z == 7)
            def _():
                for o in range(wrap + 1, 5):
                    sent_ref[o - 1, part(k)] = own(o, k)
                    pass_back(o, k).start()
                pass_cross(k).start()

        loop(forward)

        image_ref[...] = product(mine, (top_ref[0], rest_ref[0]), 1, 0)

    def move(t, k):
        arrived(t, k)
        natural(t, k).start()

    def near_sum(o, k):
        pass_on(o + 1, k).wait_recv()
        sent_ref[o - 1, part(k)] = near_ref[o, part(k)] + own(o, k)
        pass_on(o, k).start()

    def far_sum(k):
        pass_back(4, k).wait_recv()
        sent_ref[4, part(k)] = far_ref[4, part(k)] + own(5, k)
        pass_cross(k).start()

    def sideways(k):
        arrived(5, k)
        back(5, k).start()
        direct_far(k).wait_recv()
        relay(k).start()

    def plain_step(tau, k):
        if reduce_too and tau <= 4:
            o = 5 - tau
            if o + 1 <= wrap:
                near_sum(o, k)
            else:
                @pl.when(z >= 1)
                def _():
                    near_sum(o, k)

                @pl.when(z == 0)
                def _():
                    sent_ref[o - 1, part(k)] = own(o, k)
                    pass_on(o, k).start()

        @pl.when(z + tau <= edge)
        def _():
            arrived(tau, k)

        if tau <= 4:
            @pl.when(goes_on(tau))
            def _():
                natural(tau, k).start()

        if not reduce_too:
            for t in {2: (5, 4), 4: (3,)}.get(tau, ()):
                @pl.when(z + t > edge)
                def _(t=t):
                    arrived(t, k)

                    @pl.when(z <= 6)
                    def _():
                        back(t, k).start()

    if reduce_too:
        @pl.when(z <= 5)
        def _():
            for tau in range(1, 6):
                loop(functools.partial(plain_step, tau))

        @pl.when(z == 6)
        def _():
            def opening(k):
                near_sum(4, k)
                move(1, k)

            loop(opening)
            loop(functools.partial(near_sum, 3))
            loop(far_sum)
            loop(functools.partial(near_sum, 2))
            loop(functools.partial(move, 2))
            loop(functools.partial(near_sum, 1))
            loop(sideways)
            loop(functools.partial(move, 3))
            loop(functools.partial(move, 4))

        @pl.when(z == 7)
        def _():
            loop(functools.partial(near_sum, 3))
            loop(functools.partial(move, 1))
            loop(functools.partial(near_sum, 2))
            loop(functools.partial(near_sum, 1))
            loop(functools.partial(move, 2))
            loop(functools.partial(move, 3))
            loop(functools.partial(arrived, 5))
            loop(functools.partial(arrived, 4))
    else:
        for tau in range(1, 6):
            loop(functools.partial(plain_step, tau))

    if reduce_too:
        loop(pick)
        total = image_ref[...]
        for slot in (1, 2):
            total += product(halves(picked_ref[slot - 1]), (top_ref[slot], rest_ref[slot]), 1, 1)
        image_ref[...] = total

        def final(k):
            pass_on(1, k).wait_recv()
            image_ref[part(k)] += near_ref[0, part(k)]

            @pl.when(sends_direct)
            def _():
                pass_cross(k).wait_recv()
                image_ref[part(k)] += cross_ref[part(k)]

        loop(final)
    else:
        loop(pick)

    def drain(k):
        natural(0, k).wait_send()

        if reduce_too:
            @pl.when(z == 6)
            def _():
                relay(k).wait_send()

        @pl.when(sends_direct)
        def _():
            direct(k).wait_send()

        for t in range(1, 5):
            @pl.when(goes_on(t))
            def _(t=t):
                natural(t, k).wait_send()

        for t in range(wrap + 1, 6):
            if t >= 2:
                @pl.when((z + t > edge) & (z <= 6))
                def _(t=t):
                    back(t, k).wait_send()

        if reduce_too:
            for o in range(1, 6):
                @pl.when(passes(o) | (z + o > edge))
                def _(o=o):
                    pass_on(o, k).wait_send()

    loop(drain)


def band_call(offsets, data, tiles, wrap, chunks, collective_id):
    reduce_too = tiles is not None
    rows, size = data.shape
    dtype = data.dtype
    sem = pltpu.SemaphoreType.DMA
    vm = pl.BlockSpec(memory_space=pltpu.VMEM)
    sm = pl.BlockSpec(memory_space=pltpu.SMEM)
    block = pltpu.VMEM((rows, size), dtype)
    five = pltpu.VMEM((5, rows, size), dtype)
    picked = jax.ShapeDtypeStruct((2, rows, size), dtype)
    base = [sem((5, chunks)), sem((5, chunks)), sem((chunks,)), sem((4, chunks))]
    if reduce_too:
        halved = pltpu.VMEM(tiles.shape, jnp.bfloat16)
        scratch = [five, block, block, halved, halved, five, five, five, block, block] + base + [
            sem((5, chunks)), sem((5, chunks)), sem((5, chunks)), sem((chunks,)), sem((chunks,)), sem((chunks,))]
        args, ins = (offsets, data, tiles), [sm, vm, vm]
        outs, specs = (jax.ShapeDtypeStruct((rows, size), dtype), picked), (vm, vm)
    else:
        scratch = [five] + base
        args, ins, outs, specs = (offsets, data), [sm, vm], picked, vm
    return pl.pallas_call(
        functools.partial(band_kernel, wrap, chunks, reduce_too),
        out_shape=outs, in_specs=ins, out_specs=specs, scratch_shapes=scratch,
        compiler_params=pltpu.CompilerParams(collective_id=collective_id, has_side_effects=True),
    )(*args)


def step_kernel(samples, offset_ref, step_ref, data_ref, image_ref, near_ref, later_ref, tiles_ref, out_ref,
               grad_ref, pair_ref, sent_ref, up_ref, down_ref,
               p_send, p_recv, u_send, u_recv, d_send, d_recv):
    me = lax.axis_index("samp")
    core = lax.rem(me, 2)
    y = me // 2
    places = lax.axis_size("samp") // 2
    rows = out_ref.shape[1]
    twin = me + 1 - 2 * core

    barrier = pltpu.get_barrier_semaphore()

    def greet(other):
        pl.semaphore_signal(barrier, inc=1, device_id={"samp": other}, device_id_type=MESH)

    greet(twin)

    @pl.when(y < places - 1)
    def _():
        greet(me + 2)

    @pl.when(y > 0)
    def _():
        greet(me - 2)

    peers = 1 + lax.min(y, 1) + lax.min(places - 1 - y, 1)
    pl.semaphore_wait(barrier, peers)

    def band(place, which):
        return pl.ds(pl.multiple_of((2 * place + which) * rows, rows), rows)

    def to_twin(place):
        return pltpu.make_async_remote_copy(
            src_ref=grad_ref.at[:, band(place, 1 - core)], dst_ref=pair_ref.at[place],
            send_sem=p_send.at[place], recv_sem=p_recv.at[place],
            device_id={"samp": twin}, device_id_type=MESH)

    def up(place):
        return pltpu.make_async_remote_copy(
            src_ref=sent_ref.at[place], dst_ref=up_ref.at[place],
            send_sem=u_send.at[place], recv_sem=u_recv.at[place],
            device_id={"samp": me + 2}, device_id_type=MESH)

    def down(place):
        return pltpu.make_async_remote_copy(
            src_ref=sent_ref.at[place], dst_ref=down_ref.at[place],
            send_sem=d_send.at[place], recv_sem=d_recv.at[place],
            device_id={"samp": me - 2}, device_id_type=MESH)

    order = []
    for j in range(places - 1):
        order += [places - 1 - j, j]
    starts = list(dict.fromkeys(order))
    width = 2 * rows
    data, image = halves(data_ref[...]), halves(image_ref[...])
    rights = [(image, data)] + [(halves(later_ref[j]), halves(near_ref[j])) for j in range(2)]
    for place in starts:
        span = slice(width * place, width * (place + 1))
        for slot, (right_image, right_data) in enumerate(rights):
            grad_ref[slot, span] = (
                product([h[:, span] for h in data], right_image, 0, 0)
                + product([h[:, span] for h in image], right_data, 0, 0))
        to_twin(place).start()

    for j in range(places - 1):
        for rising in (True, False):
            place = places - 1 - j if rising else j

            @pl.when(y < place if rising else y > place)
            def _(place=place, rising=rising):
                to_twin(place).wait_recv()
                sent_ref[place] = grad_ref[:, band(place, core)] + pair_ref[place]

                @pl.when(y > 0 if rising else y < places - 1)
                def _():
                    if rising:
                        up(place).wait_recv()
                        sent_ref[place] += up_ref[place]
                    else:
                        down(place).wait_recv()
                        sent_ref[place] += down_ref[place]

                (up if rising else down)(place).start()

    for place in range(places):
        @pl.when(y == place)
        def _(place=place):
            to_twin(place).wait_recv()
            out_ref[...] = grad_ref[:, band(place, core)] + pair_ref[place]
            if place > 0:
                up(place).wait_recv()
                out_ref[...] += up_ref[place]
            if place < places - 1:
                down(place).wait_recv()
                out_ref[...] += down_ref[place]

    step_size = step_ref[0]
    start = pl.multiple_of(me * rows, rows)
    row_ids = start + lax.broadcasted_iota(jnp.int32, out_ref.shape[1:], 0)
    on_diag = row_ids == lax.broadcasted_iota(jnp.int32, out_ref.shape[1:], 1)
    for slot in range(3):
        old = tiles_ref[slot, pl.ds(start, rows)]
        gradient = out_ref[slot] / (2.0 * samples)
        if slot == 0:
            gradient -= jnp.where(on_diag, 1.0 / jnp.where(on_diag, old, 1.0), 0.0)
        stepped = old - step_size * gradient
        bound = step_size * PENALTY
        shrunk = jnp.where(stepped > bound, stepped - bound, jnp.where(stepped < -bound, stepped + bound, 0.0))
        if slot == 0:
            shrunk = jnp.where(on_diag, stepped, shrunk)
        else:
            shrunk = shrunk * jnp.where(offset_ref[0, slot] > 0, 1.0, 0.0)
        out_ref[slot] = shrunk

    for place in range(places):
        to_twin(place).wait_send()

        @pl.when(y < place)
        def _(place=place):
            up(place).wait_send()

        @pl.when(y > place)
        def _(place=place):
            down(place).wait_send()


def step_call(offsets, step, data, image, near, later, tiles, collective_id):
    slots, size, width = tiles.shape
    count = lax.axis_size("samp")
    rows = size // count
    sem = pltpu.SemaphoreType.DMA
    vm = pl.BlockSpec(memory_space=pltpu.VMEM)
    sm = pl.BlockSpec(memory_space=pltpu.SMEM)
    places = count // 2
    buffer = pltpu.VMEM((places, slots, rows, width), data.dtype)
    return pl.pallas_call(
        functools.partial(step_kernel, data.shape[0] * count),
        out_shape=jax.ShapeDtypeStruct((slots, rows, width), data.dtype),
        in_specs=[sm, sm] + [vm] * 5, out_specs=vm,
        scratch_shapes=[pltpu.VMEM((slots, size, width), data.dtype)] + [buffer] * 4 + [sem((places,))] * 6,
        compiler_params=pltpu.CompilerParams(collective_id=collective_id, has_side_effects=True),
    )(offsets, step, data, image, near, later, tiles)


def shards(data, tiles, offsets, step):
    tiles = tiles[0]
    image, near = band_call(offsets, data, tiles, WRAP_SUMS, CHUNKS, 1)
    later = band_call(offsets, image, None, WRAP, CHUNKS, 2)
    return step_call(offsets, step, data, image, near, later, tiles, 3)[None]


def solution(mesh):
    return jax.shard_map(
        shards,
        mesh=mesh,
        in_specs=(P("samp", "var"), P("var", None, None, None), P("var", None), P()),
        out_specs=P("var", None, "samp", None),
        check_vma=False,
    )
```

```python
import functools
import jax
import jax.numpy as jnp
from jax import lax
from jax.experimental import pallas as pl
from jax.experimental.pallas import tpu as pltpu
from jax.sharding import PartitionSpec as P

BAND = 6
MESH = pl.DeviceIdType.MESH
RING = 8
WRAP_SUMS = 3
WRAP = 2
CHUNKS = 4
PENALTY = 0.05


def halves(x):
    top = x.astype(jnp.bfloat16)
    return top, (x - top.astype(jnp.float32)).astype(jnp.bfloat16)


def product(left, right, left_dim, right_dim):
    def dot(a, b):
        return lax.dot_general(a, b, (((left_dim,), (right_dim,)), ((), ())), preferred_element_type=jnp.float32)

    return dot(left[0], right[0]) + dot(left[0], right[1]) + dot(left[1], right[0])


def var_device(index):
    return {"var": index}


class SampleSum:
    def __init__(self, rows, grad_ref, pair_ref, sent_ref, up_ref, down_ref,
                 p_send, p_recv, u_send, u_recv, d_send, d_recv):
        self.me = lax.axis_index("samp")
        self.core = lax.rem(self.me, 2)
        self.y = self.me // 2
        self.places = lax.axis_size("samp") // 2
        self.twin = self.me + 1 - 2 * self.core
        self.rows = rows
        self.grad_ref, self.pair_ref, self.sent_ref = grad_ref, pair_ref, sent_ref
        self.up_ref, self.down_ref = up_ref, down_ref
        self.sems = (p_send, p_recv, u_send, u_recv, d_send, d_recv)
        order = []
        for j in range(self.places - 1):
            order += [self.places - 1 - j, j]
        self.starts = list(dict.fromkeys(order))

    def greet(self, barrier):
        def signal(other):
            pl.semaphore_signal(barrier, inc=1, device_id={"samp": other}, device_id_type=MESH)

        signal(self.twin)

        @pl.when(self.y < self.places - 1)
        def _():
            signal(self.me + 2)

        @pl.when(self.y > 0)
        def _():
            signal(self.me - 2)

        return 1 + lax.min(self.y, 1) + lax.min(self.places - 1 - self.y, 1)

    def band(self, place, which):
        return pl.ds(pl.multiple_of((2 * place + which) * self.rows, self.rows), self.rows)

    def to_twin(self, place):
        return pltpu.make_async_remote_copy(
            src_ref=self.grad_ref.at[:, self.band(place, 1 - self.core)], dst_ref=self.pair_ref.at[place],
            send_sem=self.sems[0].at[place], recv_sem=self.sems[1].at[place],
            device_id={"samp": self.twin}, device_id_type=MESH)

    def up(self, place):
        return pltpu.make_async_remote_copy(
            src_ref=self.sent_ref.at[place], dst_ref=self.up_ref.at[place],
            send_sem=self.sems[2].at[place], recv_sem=self.sems[3].at[place],
            device_id={"samp": self.me + 2}, device_id_type=MESH)

    def down(self, place):
        return pltpu.make_async_remote_copy(
            src_ref=self.sent_ref.at[place], dst_ref=self.down_ref.at[place],
            send_sem=self.sems[4].at[place], recv_sem=self.sems[5].at[place],
            device_id={"samp": self.me - 2}, device_id_type=MESH)

    def stage(self, j):
        y, places = self.y, self.places
        for rising in (True, False):
            place = places - 1 - j if rising else j

            @pl.when(y < place if rising else y > place)
            def _(place=place, rising=rising):
                self.to_twin(place).wait_recv()
                self.sent_ref[place] = self.grad_ref[:, self.band(place, self.core)] + self.pair_ref[place]

                @pl.when(y > 0 if rising else y < places - 1)
                def _():
                    if rising:
                        self.up(place).wait_recv()
                        self.sent_ref[place] += self.up_ref[place]
                    else:
                        self.down(place).wait_recv()
                        self.sent_ref[place] += self.down_ref[place]

                (self.up if rising else self.down)(place).start()

    def finish(self, out_ref):
        for place in range(self.places):
            @pl.when(self.y == place)
            def _(place=place):
                self.to_twin(place).wait_recv()
                total = self.grad_ref[:, self.band(place, self.core)] + self.pair_ref[place]
                if place > 0:
                    self.up(place).wait_recv()
                    total += self.up_ref[place]
                if place < self.places - 1:
                    self.down(place).wait_recv()
                    total += self.down_ref[place]
                out_ref[...] = total

    def drain(self):
        for place in range(self.places):
            self.to_twin(place).wait_send()

            @pl.when(self.y < place)
            def _(place=place):
                self.up(place).wait_send()

            @pl.when(self.y > place)
            def _(place=place):
                self.down(place).wait_send()


def sum_scratch(slots, size, rows, places, dtype):
    buffer = pltpu.VMEM((places, slots, rows, size), dtype)
    return [pltpu.VMEM((slots, size, size), dtype)] + [buffer] * 4 + [pltpu.SemaphoreType.DMA((places,))] * 6


def step_kernel(samples, offset_ref, step_ref, data_ref, later_ref, rest_ref, done_ref, tiles_ref, out_ref,
                old_ref, total_ref, old_sem, *refs):
    rows = out_ref.shape[1]
    half = len(refs) // 2
    sums = [SampleSum(rows, *refs[:half]), SampleSum(rows, *refs[half:])]
    start = pl.multiple_of(sums[0].me * rows, rows)
    old_copy = pltpu.make_async_copy(tiles_ref.at[:, pl.ds(start, rows)], old_ref, old_sem)
    old_copy.start()
    barrier = pltpu.get_barrier_semaphore()
    peers = sums[0].greet(barrier)
    pl.semaphore_wait(barrier, peers)

    width = 2 * rows
    data = halves(data_ref[...])
    for slot, one in enumerate(sums):
        right = halves(later_ref[slot])
        for place in one.starts:
            span = slice(width * place, width * (place + 1))
            one.grad_ref[0, span] = product([h[:, span] for h in data], right, 0, 0) + rest_ref[slot, span]
            one.to_twin(place).start()

    for j in range(sums[0].places - 1):
        for one in sums:
            one.stage(j)
    for slot, one in enumerate(sums):
        one.finish(total_ref.at[pl.ds(slot, 1)])
    old_copy.wait()

    step_size = step_ref[0]
    bound = step_size * PENALTY
    row_ids = start + lax.broadcasted_iota(jnp.int32, out_ref.shape[1:], 0)
    on_diag = row_ids == lax.broadcasted_iota(jnp.int32, out_ref.shape[1:], 1)
    for slot in range(3):
        old = old_ref[slot]
        gradient = (done_ref[0] if slot == 0 else total_ref[slot - 1]) / (2.0 * samples)
        if slot == 0:
            gradient -= jnp.where(on_diag, 1.0 / jnp.where(on_diag, old, 1.0), 0.0)
        stepped = old - step_size * gradient
        shrunk = jnp.where(stepped > bound, stepped - bound, jnp.where(stepped < -bound, stepped + bound, 0.0))
        if slot == 0:
            shrunk = jnp.where(on_diag, stepped, shrunk)
        else:
            shrunk = shrunk * jnp.where(offset_ref[0, slot] > 0, 1.0, 0.0)
        out_ref[slot] = shrunk

    for one in sums:
        one.drain()


def band_kernel(wrap, chunks, reduce_too, *refs):
    if reduce_too:
        (offset_ref, data_ref, tiles_hbm, image_ref, picked_ref,
         tiles_ref, tiles_sem,
         ahead_ref, first_ref, second_ref, top_ref, rest_ref, sent_ref, near_ref, far_ref, cross_ref, relay_ref,
         d_send, d_recv, d_direct, d_back,
         c_send, c_near, c_far, c_cross, d_hold, d_relay) = refs
    else:
        (offset_ref, data_ref, first_data_ref, first_picked_ref, picked_ref, rest_out_ref, done_ref,
         ahead_ref, d_send, d_recv, d_direct, d_back, *sum_refs) = refs
        sums = SampleSum(done_ref.shape[1], *sum_refs)
    count = lax.axis_size("var")
    me = lax.axis_index("var")
    z = lax.rem(me, RING)
    before, after = lax.rem(me + count - 1, count), lax.rem(me + 1, count)
    left5, right5 = lax.rem(me + count - 5, count), lax.rem(me + 5, count)
    left6, right6 = lax.rem(me + count - 6, count), lax.rem(me + 6, count)
    rows = data_ref.shape[0] // chunks
    edge = 7 + wrap

    if reduce_too:
        tiles_copy = pltpu.make_async_copy(tiles_hbm, tiles_ref, tiles_sem)
        tiles_copy.start()
    barrier = pltpu.get_barrier_semaphore()
    others = (before, after, left5, right5) + ((left6, right6) if reduce_too else ())
    for other in others:
        pl.semaphore_signal(barrier, inc=1, device_id=var_device(other), device_id_type=MESH)
    greeted = len(others)
    if not reduce_too:
        greeted = greeted + sums.greet(barrier)
    pl.semaphore_wait(barrier, greeted)

    def part(k):
        return pl.ds(pl.multiple_of(k * rows, rows), rows)

    def natural(t, k):
        source = data_ref.at[part(k)] if t == 0 else ahead_ref.at[t - 1, part(k)]
        return pltpu.make_async_remote_copy(
            src_ref=source, dst_ref=ahead_ref.at[t, part(k)],
            send_sem=d_send.at[t, k], recv_sem=d_recv.at[t, k],
            device_id=var_device(before), device_id_type=MESH)

    def direct(k):
        return pltpu.make_async_remote_copy(
            src_ref=data_ref.at[part(k)], dst_ref=ahead_ref.at[4, part(k)],
            send_sem=d_direct.at[k], recv_sem=d_recv.at[4, k],
            device_id=var_device(left5), device_id_type=MESH)

    def direct_far(k):
        return pltpu.make_async_remote_copy(
            src_ref=data_ref.at[part(k)], dst_ref=relay_ref.at[part(k)],
            send_sem=d_direct.at[k], recv_sem=d_hold.at[k],
            device_id=var_device(left6), device_id_type=MESH)

    def relay(k):
        return pltpu.make_async_remote_copy(
            src_ref=relay_ref.at[part(k)], dst_ref=ahead_ref.at[4, part(k)],
            send_sem=d_relay.at[k], recv_sem=d_recv.at[4, k],
            device_id=var_device(after), device_id_type=MESH)

    def back(t, k):
        return pltpu.make_async_remote_copy(
            src_ref=ahead_ref.at[t - 1, part(k)], dst_ref=ahead_ref.at[t - 2, part(k)],
            send_sem=d_back.at[t - 2, k], recv_sem=d_recv.at[t - 2, k],
            device_id=var_device(after), device_id_type=MESH)

    def goes_on(t):
        return ((z >= 1) & (z + t <= edge)) | ((z == 0) & (t + 1 <= wrap))

    sends_direct = (z >= wrap) & (z <= 4)

    def arrived(t, k):
        natural(t - 1, k).wait_recv()

    def chosen(slot, o):
        return jnp.where(offset_ref[0, slot] == o, 1.0, 0.0)

    def own(o, k):
        return chosen(1, o) * first_ref[part(k)] + chosen(2, o) * second_ref[part(k)]

    def pick(k):
        for slot in (1, 2):
            block = chosen(slot, 1) * ahead_ref[0, part(k)]
            for o in range(2, BAND):
                block += chosen(slot, o) * ahead_ref[o - 1, part(k)]
            picked_ref[slot - 1, part(k)] = block

    def pass_on(o, k):
        return pltpu.make_async_remote_copy(
            src_ref=sent_ref.at[o - 1, part(k)], dst_ref=near_ref.at[o - 1, part(k)],
            send_sem=c_send.at[o - 1, k], recv_sem=c_near.at[o - 1, k],
            device_id=var_device(after), device_id_type=MESH)

    def pass_back(o, k):
        return pltpu.make_async_remote_copy(
            src_ref=sent_ref.at[o - 1, part(k)], dst_ref=far_ref.at[o, part(k)],
            send_sem=c_send.at[o - 1, k], recv_sem=c_far.at[o, k],
            device_id=var_device(before), device_id_type=MESH)

    def pass_cross(k):
        return pltpu.make_async_remote_copy(
            src_ref=sent_ref.at[4, part(k)], dst_ref=cross_ref.at[part(k)],
            send_sem=c_send.at[4, k], recv_sem=c_cross.at[k],
            device_id=var_device(right5), device_id_type=MESH)

    def passes(o):
        return ((z <= 6) & (z + o <= edge)) | ((z == 7) & (o <= wrap))

    def loop(body):
        def step(k, carry):
            body(k)
            return carry
        lax.fori_loop(0, chunks, step, 0)

    def first(k):
        natural(0, k).start()

        if reduce_too:
            @pl.when((z >= wrap) & (z <= 3))
            def _():
                direct(k).start()

            @pl.when(z == 4)
            def _():
                direct_far(k).start()
        else:
            @pl.when(sends_direct)
            def _():
                direct(k).start()

    loop(first)

    if reduce_too:
        tiles_copy.wait()
        for slot in range(3):
            top, rest = halves(tiles_ref[slot])
            top_ref[slot] = top
            rest_ref[slot] = rest

        mine = halves(data_ref[...])
        first_ref[...] = product(mine, (top_ref[1], rest_ref[1]), 1, 0)
        second_ref[...] = product(mine, (top_ref[2], rest_ref[2]), 1, 0)

        def forward(k):
            sent_ref[4, part(k)] = own(5, k)

            @pl.when(passes(5))
            def _():
                pass_on(5, k).start()

            @pl.when(z == 7)
            def _():
                for o in range(wrap + 1, 5):
                    sent_ref[o - 1, part(k)] = own(o, k)
                    pass_back(o, k).start()
                pass_cross(k).start()

        loop(forward)

        image_ref[...] = product(mine, (top_ref[0], rest_ref[0]), 1, 0)

    def move(t, k):
        arrived(t, k)
        natural(t, k).start()

    def near_sum(o, k):
        pass_on(o + 1, k).wait_recv()
        sent_ref[o - 1, part(k)] = near_ref[o, part(k)] + own(o, k)
        pass_on(o, k).start()

    def far_sum(k):
        pass_back(4, k).wait_recv()
        sent_ref[4, part(k)] = far_ref[4, part(k)] + own(5, k)
        pass_cross(k).start()

    def sideways(k):
        arrived(5, k)
        back(5, k).start()
        direct_far(k).wait_recv()
        relay(k).start()

    def plain_step(tau, k):
        if reduce_too and tau <= 4:
            o = 5 - tau
            if o + 1 <= wrap:
                near_sum(o, k)
            else:
                @pl.when(z >= 1)
                def _():
                    near_sum(o, k)

                @pl.when(z == 0)
                def _():
                    sent_ref[o - 1, part(k)] = own(o, k)
                    pass_on(o, k).start()

        @pl.when(z + tau <= edge)
        def _():
            arrived(tau, k)

        if tau <= 4:
            @pl.when(goes_on(tau))
            def _():
                natural(tau, k).start()

        if not reduce_too:
            for t in {2: (5, 4), 4: (3,)}.get(tau, ()):
                @pl.when(z + t > edge)
                def _(t=t):
                    arrived(t, k)

                    @pl.when(z <= 6)
                    def _():
                        back(t, k).start()

    if reduce_too:
        @pl.when(z <= 5)
        def _():
            for tau in range(1, 6):
                loop(functools.partial(plain_step, tau))

        @pl.when(z == 6)
        def _():
            def opening(k):
                near_sum(4, k)
                move(1, k)

            loop(opening)
            loop(functools.partial(near_sum, 3))
            loop(far_sum)
            loop(functools.partial(near_sum, 2))
            loop(functools.partial(move, 2))
            loop(functools.partial(near_sum, 1))
            loop(sideways)
            loop(functools.partial(move, 3))
            loop(functools.partial(move, 4))

        @pl.when(z == 7)
        def _():
            loop(functools.partial(near_sum, 3))
            loop(functools.partial(move, 1))
            loop(functools.partial(near_sum, 2))
            loop(functools.partial(near_sum, 1))
            loop(functools.partial(move, 2))
            loop(functools.partial(move, 3))
            loop(functools.partial(arrived, 5))
            loop(functools.partial(arrived, 4))
    else:
        image, data = halves(data_ref[...]), halves(first_data_ref[...])
        sums.grad_ref[0] = product(data, image, 0, 0) + product(image, data, 0, 0)
        for place in sums.starts:
            sums.to_twin(place).start()
        for slot in range(2):
            rest_out_ref[slot] = product(image, halves(first_picked_ref[slot]), 0, 0)
        for tau in range(1, 6):
            loop(functools.partial(plain_step, tau))
            for j in range(3):
                if tau == (3, 4, 5)[j]:
                    sums.stage(j)

    if reduce_too:
        loop(pick)
        total = image_ref[...]
        for slot in (1, 2):
            total += product(halves(picked_ref[slot - 1]), (top_ref[slot], rest_ref[slot]), 1, 1)
        image_ref[...] = total

        def final(k):
            pass_on(1, k).wait_recv()
            image_ref[part(k)] += near_ref[0, part(k)]

            @pl.when(sends_direct)
            def _():
                pass_cross(k).wait_recv()
                image_ref[part(k)] += cross_ref[part(k)]

        loop(final)
    else:
        loop(pick)
        sums.finish(done_ref)
        sums.drain()

    def drain(k):
        natural(0, k).wait_send()

        if reduce_too:
            @pl.when(z == 6)
            def _():
                relay(k).wait_send()

        @pl.when(sends_direct)
        def _():
            direct(k).wait_send()

        for t in range(1, 5):
            @pl.when(goes_on(t))
            def _(t=t):
                natural(t, k).wait_send()

        for t in range(wrap + 1, 6):
            if t >= 2:
                @pl.when((z + t > edge) & (z <= 6))
                def _(t=t):
                    back(t, k).wait_send()

        if reduce_too:
            for o in range(1, 6):
                @pl.when(passes(o) | (z + o > edge))
                def _(o=o):
                    pass_on(o, k).wait_send()

    loop(drain)


def band_call(offsets, data, tiles, earlier, wrap, chunks, collective_id):
    reduce_too = tiles is not None
    rows, size = data.shape
    dtype = data.dtype
    sem = pltpu.SemaphoreType.DMA
    vm = pl.BlockSpec(memory_space=pltpu.VMEM)
    sm = pl.BlockSpec(memory_space=pltpu.SMEM)
    block = pltpu.VMEM((rows, size), dtype)
    five = pltpu.VMEM((5, rows, size), dtype)
    picked = jax.ShapeDtypeStruct((2, rows, size), dtype)
    base = [sem((5, chunks)), sem((5, chunks)), sem((chunks,)), sem((4, chunks))]
    if reduce_too:
        halved = pltpu.VMEM(tiles.shape, jnp.bfloat16)
        scratch = [pltpu.VMEM(tiles.shape, dtype), sem, five, block, block, halved, halved, five, five, five, block, block] + base + [
            sem((5, chunks)), sem((5, chunks)), sem((5, chunks)), sem((chunks,)), sem((chunks,)), sem((chunks,))]
        args, ins = (offsets, data, tiles), [sm, vm, pl.BlockSpec(memory_space=pl.ANY)]
        outs, specs = (jax.ShapeDtypeStruct((rows, size), dtype), picked), (vm, vm)
    else:
        count = lax.axis_size("samp")
        scratch = [five] + base + sum_scratch(1, size, size // count, count // 2, dtype)
        args, ins = (offsets, data, *earlier), [sm, vm, vm, vm]
        outs = (picked, jax.ShapeDtypeStruct((2, size, size), dtype), jax.ShapeDtypeStruct((1, size // count, size), dtype))
        specs = (vm, vm, vm)
    return pl.pallas_call(
        functools.partial(band_kernel, wrap, chunks, reduce_too),
        out_shape=outs, in_specs=ins, out_specs=specs, scratch_shapes=scratch,
        compiler_params=pltpu.CompilerParams(collective_id=collective_id, has_side_effects=True),
    )(*args)


def step_call(offsets, step, data, later, rest, done, tiles, collective_id):
    slots, size, width = tiles.shape
    count = lax.axis_size("samp")
    rows = size // count
    vm = pl.BlockSpec(memory_space=pltpu.VMEM)
    sm = pl.BlockSpec(memory_space=pltpu.SMEM)
    dtype = data.dtype
    return pl.pallas_call(
        functools.partial(step_kernel, data.shape[0] * count),
        out_shape=jax.ShapeDtypeStruct((slots, rows, width), dtype),
        in_specs=[sm, sm] + [vm] * 4 + [pl.BlockSpec(memory_space=pl.ANY)], out_specs=vm,
        scratch_shapes=[pltpu.VMEM((slots, rows, width), dtype), pltpu.VMEM((2, rows, width), dtype),
                        pltpu.SemaphoreType.DMA] + sum_scratch(1, size, rows, count // 2, dtype) * 2,
        compiler_params=pltpu.CompilerParams(collective_id=collective_id, has_side_effects=True),
    )(offsets, step, data, later, rest, done, tiles)


def shards(data, tiles, offsets, step):
    tiles = tiles[0]
    image, near = band_call(offsets, data, tiles, None, WRAP_SUMS, CHUNKS, 1)
    later, rest, done = band_call(offsets, image, None, (data, near), WRAP, CHUNKS, 2)
    return step_call(offsets, step, data, later, rest, done, tiles, 3)[None]


def solution(mesh):
    return jax.shard_map(
        shards,
        mesh=mesh,
        in_specs=(P("samp", "var"), P("var", None, None, None), P("var", None), P()),
        out_specs=P("var", None, "samp", None),
        check_vma=False,
    )
```

```python
import functools
import jax
import jax.numpy as jnp
from jax import lax
from jax.experimental import pallas as pl
from jax.experimental.pallas import tpu as pltpu
from jax.sharding import PartitionSpec as P

BAND = 6
MESH = pl.DeviceIdType.MESH
RING = 8
WRAP_SUMS = 3
WRAP = 2
CHUNKS = 4
PENALTY = 0.05


def halves(x):
    top = x.astype(jnp.bfloat16)
    return top, (x - top.astype(jnp.float32)).astype(jnp.bfloat16)


def product(left, right, left_dim, right_dim):
    def dot(a, b):
        return lax.dot_general(a, b, (((left_dim,), (right_dim,)), ((), ())), preferred_element_type=jnp.float32)

    return dot(left[0], right[0]) + dot(left[0], right[1]) + dot(left[1], right[0])


def var_device(index):
    return {"var": index}


class SampleSum:
    def __init__(self, rows, grad_ref, pair_ref, sent_ref, up_ref, down_ref,
                 p_send, p_recv, u_send, u_recv, d_send, d_recv):
        self.me = lax.axis_index("samp")
        self.core = lax.rem(self.me, 2)
        self.y = self.me // 2
        self.places = lax.axis_size("samp") // 2
        self.twin = self.me + 1 - 2 * self.core
        self.rows = rows
        self.grad_ref, self.pair_ref, self.sent_ref = grad_ref, pair_ref, sent_ref
        self.up_ref, self.down_ref = up_ref, down_ref
        self.sems = (p_send, p_recv, u_send, u_recv, d_send, d_recv)
        order = []
        for j in range(self.places - 1):
            order += [self.places - 1 - j, j]
        self.starts = list(dict.fromkeys(order))

    def greet(self, barrier):
        def signal(other):
            pl.semaphore_signal(barrier, inc=1, device_id={"samp": other}, device_id_type=MESH)

        signal(self.twin)

        @pl.when(self.y < self.places - 1)
        def _():
            signal(self.me + 2)

        @pl.when(self.y > 0)
        def _():
            signal(self.me - 2)

        return 1 + lax.min(self.y, 1) + lax.min(self.places - 1 - self.y, 1)

    def band(self, place, which):
        return pl.ds(pl.multiple_of((2 * place + which) * self.rows, self.rows), self.rows)

    def to_twin(self, place):
        return pltpu.make_async_remote_copy(
            src_ref=self.grad_ref.at[:, self.band(place, 1 - self.core)], dst_ref=self.pair_ref.at[place],
            send_sem=self.sems[0].at[place], recv_sem=self.sems[1].at[place],
            device_id={"samp": self.twin}, device_id_type=MESH)

    def up(self, place):
        return pltpu.make_async_remote_copy(
            src_ref=self.sent_ref.at[place], dst_ref=self.up_ref.at[place],
            send_sem=self.sems[2].at[place], recv_sem=self.sems[3].at[place],
            device_id={"samp": self.me + 2}, device_id_type=MESH)

    def down(self, place):
        return pltpu.make_async_remote_copy(
            src_ref=self.sent_ref.at[place], dst_ref=self.down_ref.at[place],
            send_sem=self.sems[4].at[place], recv_sem=self.sems[5].at[place],
            device_id={"samp": self.me - 2}, device_id_type=MESH)

    def stage(self, j):
        y, places = self.y, self.places
        for rising in (True, False):
            place = places - 1 - j if rising else j

            @pl.when(y < place if rising else y > place)
            def _(place=place, rising=rising):
                self.to_twin(place).wait_recv()
                self.sent_ref[place] = self.grad_ref[:, self.band(place, self.core)] + self.pair_ref[place]

                @pl.when(y > 0 if rising else y < places - 1)
                def _():
                    if rising:
                        self.up(place).wait_recv()
                        self.sent_ref[place] += self.up_ref[place]
                    else:
                        self.down(place).wait_recv()
                        self.sent_ref[place] += self.down_ref[place]

                (self.up if rising else self.down)(place).start()

    def finish(self, out_ref):
        for place in range(self.places):
            @pl.when(self.y == place)
            def _(place=place):
                self.to_twin(place).wait_recv()
                total = self.grad_ref[:, self.band(place, self.core)] + self.pair_ref[place]
                if place > 0:
                    self.up(place).wait_recv()
                    total += self.up_ref[place]
                if place < self.places - 1:
                    self.down(place).wait_recv()
                    total += self.down_ref[place]
                out_ref[...] = total

    def drain(self):
        for place in range(self.places):
            self.to_twin(place).wait_send()

            @pl.when(self.y < place)
            def _(place=place):
                self.up(place).wait_send()

            @pl.when(self.y > place)
            def _(place=place):
                self.down(place).wait_send()


def sum_scratch(slots, size, rows, places, dtype):
    buffer = pltpu.VMEM((places, slots, rows, size), dtype)
    return [pltpu.VMEM((slots, size, size), dtype)] + [buffer] * 4 + [pltpu.SemaphoreType.DMA((places,))] * 6


def step_kernel(samples, offset_ref, step_ref, data_ref, later_ref, rest_ref, done_ref, tiles_ref, out_ref,
                old_ref, total_ref, old_sem, *refs):
    rows = out_ref.shape[1]
    half = len(refs) // 2
    sums = [SampleSum(rows, *refs[:half]), SampleSum(rows, *refs[half:])]
    start = pl.multiple_of(sums[0].me * rows, rows)
    old_copy = pltpu.make_async_copy(tiles_ref.at[:, pl.ds(start, rows)], old_ref, old_sem)
    old_copy.start()
    barrier = pltpu.get_barrier_semaphore()
    peers = sums[0].greet(barrier)
    pl.semaphore_wait(barrier, peers)

    width = 2 * rows
    data = halves(data_ref[...])
    for slot, one in enumerate(sums):
        right = halves(later_ref[slot])
        for place in one.starts:
            span = slice(width * place, width * (place + 1))
            one.grad_ref[0, span] = product([h[:, span] for h in data], right, 0, 0) + rest_ref[slot, span]
            one.to_twin(place).start()

    for j in range(sums[0].places - 1):
        for one in sums:
            one.stage(j)
    for slot, one in enumerate(sums):
        one.finish(total_ref.at[pl.ds(slot, 1)])
    old_copy.wait()

    step_size = step_ref[0]
    bound = step_size * PENALTY
    row_ids = start + lax.broadcasted_iota(jnp.int32, out_ref.shape[1:], 0)
    on_diag = row_ids == lax.broadcasted_iota(jnp.int32, out_ref.shape[1:], 1)
    for slot in range(3):
        old = old_ref[slot]
        gradient = (done_ref[0] if slot == 0 else total_ref[slot - 1]) / (2.0 * samples)
        if slot == 0:
            gradient -= jnp.where(on_diag, 1.0 / jnp.where(on_diag, old, 1.0), 0.0)
        stepped = old - step_size * gradient
        shrunk = jnp.where(stepped > bound, stepped - bound, jnp.where(stepped < -bound, stepped + bound, 0.0))
        if slot == 0:
            shrunk = jnp.where(on_diag, stepped, shrunk)
        else:
            shrunk = shrunk * jnp.where(offset_ref[0, slot] > 0, 1.0, 0.0)
        out_ref[slot] = shrunk

    for one in sums:
        one.drain()


def band_kernel(wrap, chunks, reduce_too, *refs):
    if reduce_too:
        (offset_ref, data_ref, tiles_hbm, image_ref, picked_ref,
         tiles_ref, tiles_sem,
         ahead_ref, first_ref, second_ref, top_ref, rest_ref, sent_ref, near_ref, far_ref, cross_ref, relay_ref,
         d_send, d_recv, d_direct, d_back,
         c_send, c_near, c_far, c_cross, d_hold, d_relay) = refs
    else:
        (offset_ref, data_ref, first_data_ref, first_picked_ref, picked_ref, rest_out_ref, done_ref,
         ahead_ref, d_send, d_recv, d_direct, d_back, *sum_refs) = refs
        sums = SampleSum(done_ref.shape[1], *sum_refs)
    count = lax.axis_size("var")
    me = lax.axis_index("var")
    z = lax.rem(me, RING)
    before, after = lax.rem(me + count - 1, count), lax.rem(me + 1, count)
    left5, right5 = lax.rem(me + count - 5, count), lax.rem(me + 5, count)
    left6, right6 = lax.rem(me + count - 6, count), lax.rem(me + 6, count)
    rows = data_ref.shape[0] // chunks
    edge = 7 + wrap

    if reduce_too:
        tiles_copy = pltpu.make_async_copy(tiles_hbm, tiles_ref, tiles_sem)
        tiles_copy.start()
    barrier = pltpu.get_barrier_semaphore()
    others = (before, after, left5, right5) + ((left6, right6) if reduce_too else ())
    for other in others:
        pl.semaphore_signal(barrier, inc=1, device_id=var_device(other), device_id_type=MESH)
    greeted = len(others)
    if not reduce_too:
        greeted = greeted + sums.greet(barrier)
    pl.semaphore_wait(barrier, greeted)

    def part(k):
        return pl.ds(pl.multiple_of(k * rows, rows), rows)

    def natural(t, k):
        source = data_ref.at[part(k)] if t == 0 else ahead_ref.at[t - 1, part(k)]
        return pltpu.make_async_remote_copy(
            src_ref=source, dst_ref=ahead_ref.at[t, part(k)],
            send_sem=d_send.at[t, k], recv_sem=d_recv.at[t, k],
            device_id=var_device(before), device_id_type=MESH)

    def direct(k):
        return pltpu.make_async_remote_copy(
            src_ref=data_ref.at[part(k)], dst_ref=ahead_ref.at[4, part(k)],
            send_sem=d_direct.at[k], recv_sem=d_recv.at[4, k],
            device_id=var_device(left5), device_id_type=MESH)

    def direct_far(k):
        return pltpu.make_async_remote_copy(
            src_ref=data_ref.at[part(k)], dst_ref=relay_ref.at[part(k)],
            send_sem=d_direct.at[k], recv_sem=d_hold.at[k],
            device_id=var_device(left6), device_id_type=MESH)

    def relay(k):
        return pltpu.make_async_remote_copy(
            src_ref=relay_ref.at[part(k)], dst_ref=ahead_ref.at[4, part(k)],
            send_sem=d_relay.at[k], recv_sem=d_recv.at[4, k],
            device_id=var_device(after), device_id_type=MESH)

    def back(t, k):
        return pltpu.make_async_remote_copy(
            src_ref=ahead_ref.at[t - 1, part(k)], dst_ref=ahead_ref.at[t - 2, part(k)],
            send_sem=d_back.at[t - 2, k], recv_sem=d_recv.at[t - 2, k],
            device_id=var_device(after), device_id_type=MESH)

    def goes_on(t):
        return ((z >= 1) & (z + t <= edge)) | ((z == 0) & (t + 1 <= wrap))

    sends_direct = (z >= wrap) & (z <= 4)

    def arrived(t, k):
        natural(t - 1, k).wait_recv()

    def chosen(slot, o):
        return jnp.where(offset_ref[0, slot] == o, 1.0, 0.0)

    def own(o, k):
        return chosen(1, o) * first_ref[part(k)] + chosen(2, o) * second_ref[part(k)]

    def pick(k):
        for slot in (1, 2):
            block = chosen(slot, 1) * ahead_ref[0, part(k)]
            for o in range(2, BAND):
                block += chosen(slot, o) * ahead_ref[o - 1, part(k)]
            picked_ref[slot - 1, part(k)] = block

    def pass_on(o, k):
        return pltpu.make_async_remote_copy(
            src_ref=sent_ref.at[o - 1, part(k)], dst_ref=near_ref.at[o - 1, part(k)],
            send_sem=c_send.at[o - 1, k], recv_sem=c_near.at[o - 1, k],
            device_id=var_device(after), device_id_type=MESH)

    def pass_back(o, k):
        return pltpu.make_async_remote_copy(
            src_ref=sent_ref.at[o - 1, part(k)], dst_ref=far_ref.at[o, part(k)],
            send_sem=c_send.at[o - 1, k], recv_sem=c_far.at[o, k],
            device_id=var_device(before), device_id_type=MESH)

    def pass_cross(k):
        return pltpu.make_async_remote_copy(
            src_ref=sent_ref.at[4, part(k)], dst_ref=cross_ref.at[part(k)],
            send_sem=c_send.at[4, k], recv_sem=c_cross.at[k],
            device_id=var_device(right5), device_id_type=MESH)

    def passes(o):
        return ((z <= 6) & (z + o <= edge)) | ((z == 7) & (o <= wrap))

    def loop(body):
        def step(k, carry):
            body(k)
            return carry
        lax.fori_loop(0, chunks, step, 0)

    def first(k):
        natural(0, k).start()

        if reduce_too:
            @pl.when((z >= wrap) & (z <= 3))
            def _():
                direct(k).start()

        else:
            @pl.when(sends_direct)
            def _():
                direct(k).start()

    loop(first)

    if reduce_too:
        tiles_copy.wait()
        for slot in range(3):
            top, rest = halves(tiles_ref[slot])
            top_ref[slot] = top
            rest_ref[slot] = rest

        mine = halves(data_ref[...])
        first_ref[...] = product(mine, (top_ref[1], rest_ref[1]), 1, 0)
        second_ref[...] = product(mine, (top_ref[2], rest_ref[2]), 1, 0)

        def forward(k):
            sent_ref[4, part(k)] = own(5, k)

            @pl.when(passes(5))
            def _():
                pass_on(5, k).start()

            @pl.when(z == 7)
            def _():
                for o in range(wrap + 1, 5):
                    sent_ref[o - 1, part(k)] = own(o, k)
                    pass_back(o, k).start()
                pass_cross(k).start()

        loop(forward)

        image_ref[...] = product(mine, (top_ref[0], rest_ref[0]), 1, 0)

    def move(t, k):
        arrived(t, k)
        natural(t, k).start()

    def near_sum(o, k):
        pass_on(o + 1, k).wait_recv()
        sent_ref[o - 1, part(k)] = near_ref[o, part(k)] + own(o, k)
        pass_on(o, k).start()

    def far_sum(k):
        pass_back(4, k).wait_recv()
        sent_ref[4, part(k)] = far_ref[4, part(k)] + own(5, k)
        pass_cross(k).start()

    def sideways(k):
        arrived(5, k)
        back(5, k).start()
        direct_far(k).wait_recv()
        relay(k).start()

    def plain_step(tau, k):
        if reduce_too and tau <= 4:
            o = 5 - tau
            if o + 1 <= wrap:
                near_sum(o, k)
            else:
                @pl.when(z >= 1)
                def _():
                    near_sum(o, k)

                @pl.when(z == 0)
                def _():
                    sent_ref[o - 1, part(k)] = own(o, k)
                    pass_on(o, k).start()

        @pl.when(z + tau <= edge)
        def _():
            arrived(tau, k)

        if tau <= 4:
            @pl.when(goes_on(tau))
            def _():
                natural(tau, k).start()

        if not reduce_too:
            for t in {2: (5, 4), 4: (3,)}.get(tau, ()):
                @pl.when(z + t > edge)
                def _(t=t):
                    arrived(t, k)

                    @pl.when(z <= 6)
                    def _():
                        back(t, k).start()

    if reduce_too:
        @pl.when(z <= 5)
        def _():
            for tau in range(1, 6):
                if tau == 3:
                    @pl.when(z == 4)
                    def _():
                        loop(lambda k: direct_far(k).start())

                loop(functools.partial(plain_step, tau))

        @pl.when(z == 6)
        def _():
            def opening(k):
                near_sum(4, k)
                move(1, k)

            loop(opening)
            loop(functools.partial(near_sum, 3))
            loop(far_sum)
            loop(functools.partial(near_sum, 2))
            loop(functools.partial(move, 2))
            loop(functools.partial(near_sum, 1))
            loop(sideways)
            loop(functools.partial(move, 3))
            loop(functools.partial(move, 4))

        @pl.when(z == 7)
        def _():
            loop(functools.partial(near_sum, 3))
            loop(functools.partial(move, 1))
            loop(functools.partial(near_sum, 2))
            loop(functools.partial(near_sum, 1))
            loop(functools.partial(move, 2))
            loop(functools.partial(move, 3))
            loop(functools.partial(arrived, 5))
            loop(functools.partial(arrived, 4))
    else:
        image, data = halves(data_ref[...]), halves(first_data_ref[...])
        sums.grad_ref[0] = product(data, image, 0, 0) + product(image, data, 0, 0)
        for place in sums.starts:
            sums.to_twin(place).start()
        for slot in range(2):
            rest_out_ref[slot] = product(image, halves(first_picked_ref[slot]), 0, 0)
        for tau in range(1, 6):
            loop(functools.partial(plain_step, tau))
            for j in range(3):
                if tau == (3, 4, 5)[j]:
                    sums.stage(j)

    if reduce_too:
        loop(pick)
        total = image_ref[...]
        for slot in (1, 2):
            total += product(halves(picked_ref[slot - 1]), (top_ref[slot], rest_ref[slot]), 1, 1)
        image_ref[...] = total

        def final(k):
            pass_on(1, k).wait_recv()
            image_ref[part(k)] += near_ref[0, part(k)]

            @pl.when(sends_direct)
            def _():
                pass_cross(k).wait_recv()
                image_ref[part(k)] += cross_ref[part(k)]

        loop(final)
    else:
        loop(pick)
        sums.finish(done_ref)
        sums.drain()

    def drain(k):
        natural(0, k).wait_send()

        if reduce_too:
            @pl.when(z == 6)
            def _():
                relay(k).wait_send()

        @pl.when(sends_direct)
        def _():
            direct(k).wait_send()

        for t in range(1, 5):
            @pl.when(goes_on(t))
            def _(t=t):
                natural(t, k).wait_send()

        for t in range(wrap + 1, 6):
            if t >= 2:
                @pl.when((z + t > edge) & (z <= 6))
                def _(t=t):
                    back(t, k).wait_send()

        if reduce_too:
            for o in range(1, 6):
                @pl.when(passes(o) | (z + o > edge))
                def _(o=o):
                    pass_on(o, k).wait_send()

    loop(drain)


def band_call(offsets, data, tiles, earlier, wrap, chunks, collective_id):
    reduce_too = tiles is not None
    rows, size = data.shape
    dtype = data.dtype
    sem = pltpu.SemaphoreType.DMA
    vm = pl.BlockSpec(memory_space=pltpu.VMEM)
    sm = pl.BlockSpec(memory_space=pltpu.SMEM)
    block = pltpu.VMEM((rows, size), dtype)
    five = pltpu.VMEM((5, rows, size), dtype)
    picked = jax.ShapeDtypeStruct((2, rows, size), dtype)
    base = [sem((5, chunks)), sem((5, chunks)), sem((chunks,)), sem((4, chunks))]
    if reduce_too:
        halved = pltpu.VMEM(tiles.shape, jnp.bfloat16)
        scratch = [pltpu.VMEM(tiles.shape, dtype), sem, five, block, block, halved, halved, five, five, five, block, block] + base + [
            sem((5, chunks)), sem((5, chunks)), sem((5, chunks)), sem((chunks,)), sem((chunks,)), sem((chunks,))]
        args, ins = (offsets, data, tiles), [sm, vm, pl.BlockSpec(memory_space=pl.ANY)]
        outs, specs = (jax.ShapeDtypeStruct((rows, size), dtype), picked), (vm, vm)
    else:
        count = lax.axis_size("samp")
        scratch = [five] + base + sum_scratch(1, size, size // count, count // 2, dtype)
        args, ins = (offsets, data, *earlier), [sm, vm, vm, vm]
        outs = (picked, jax.ShapeDtypeStruct((2, size, size), dtype), jax.ShapeDtypeStruct((1, size // count, size), dtype))
        specs = (vm, vm, vm)
    return pl.pallas_call(
        functools.partial(band_kernel, wrap, chunks, reduce_too),
        out_shape=outs, in_specs=ins, out_specs=specs, scratch_shapes=scratch,
        compiler_params=pltpu.CompilerParams(collective_id=collective_id, has_side_effects=True),
    )(*args)


def step_call(offsets, step, data, later, rest, done, tiles, collective_id):
    slots, size, width = tiles.shape
    count = lax.axis_size("samp")
    rows = size // count
    vm = pl.BlockSpec(memory_space=pltpu.VMEM)
    sm = pl.BlockSpec(memory_space=pltpu.SMEM)
    dtype = data.dtype
    return pl.pallas_call(
        functools.partial(step_kernel, data.shape[0] * count),
        out_shape=jax.ShapeDtypeStruct((slots, rows, width), dtype),
        in_specs=[sm, sm] + [vm] * 4 + [pl.BlockSpec(memory_space=pl.ANY)], out_specs=vm,
        scratch_shapes=[pltpu.VMEM((slots, rows, width), dtype), pltpu.VMEM((2, rows, width), dtype),
                        pltpu.SemaphoreType.DMA] + sum_scratch(1, size, rows, count // 2, dtype) * 2,
        compiler_params=pltpu.CompilerParams(collective_id=collective_id, has_side_effects=True),
    )(offsets, step, data, later, rest, done, tiles)


def shards(data, tiles, offsets, step):
    tiles = tiles[0]
    image, near = band_call(offsets, data, tiles, None, WRAP_SUMS, CHUNKS, 1)
    later, rest, done = band_call(offsets, image, None, (data, near), WRAP, CHUNKS, 2)
    return step_call(offsets, step, data, later, rest, done, tiles, 3)[None]


def solution(mesh):
    return jax.shard_map(
        shards,
        mesh=mesh,
        in_specs=(P("samp", "var"), P("var", None, None, None), P("var", None), P()),
        out_specs=P("var", None, "samp", None),
        check_vma=False,
    )
```
